32 devices in a mesh: grp: 2 (over x), gene: 4 (over y, core), cell: 4 (over z).
Axes of the slice: x: 2, y: 2, z: 4, core: 2. Of those that a mesh axis runs over, the one named last changes fastest.
Arguments:
- data: bfloat16 [2, 15360, 1024], P('grp', 'gene', 'cell'), may hold values from 0 to 48
- shared_w: float32 [15360, 256], P(('gene', 'cell')), may hold values from 0.002 to 2
- specific_v: float32 [2, 15360, 256], P('grp', ('gene', 'cell')), may hold values from 0.0005 to 0.5
- factor_h: float32 [2, 256, 1024], P('grp', None, 'cell'), may hold values from 0.01 to 1
- cell_count: int32 [2], P('grp'), may hold values from 256 to 1024, as said below
Outputs:
- new_w: float32 [15360, 256], P(('gene', 'cell'))
- new_v: float32 [2, 15360, 256], P('grp', ('gene', 'cell'))
- new_h: float32 [2, 256, 1024], P('grp', None, 'cell')
The draws below stay inside these ranges and needn't reach their ends.
Inputs may be any that keep to these rules, and one draw needn't show every extreme that they name: `cell_count`: in each draw one dataset, chosen from the seed, has all 1024 cell slots live and the other between 256 and 512; the live slots are the first ones.
All inputs are finite; a program needn't handle non-finite values.
Results may differ from the reference program's by a relative error of at most 0.0044.
Values may be sent and summed in bfloat16 or wider, within the bound.
No kernel may reach another device: no remote copies, remote signals or barrier semaphores. Data moves between devices by JAX's collectives and lax.ppermute only.
A program may use at most 64 MiB of HBM per device.

```python
import math
import jax
import jax.numpy as jnp
from jax import lax

G = 15360
K = 256
KB = 32
SWEEPS = 4
NC = 1024


def draw_cell_count(key, part):
    first, second = jax.random.split(jax.random.fold_in(key, 17))
    small = jax.random.randint(first, (), NC // 4, NC // 2 + 1, dtype=jnp.int32)
    which = jax.random.randint(second, (), 0, 2, dtype=jnp.int32)
    full = jnp.full((), NC, jnp.int32)
    return jnp.stack([jnp.where(which == 0, full, small), jnp.where(which == 0, small, full)])


def level_of(stream_key, dims, shards, least, top_value):
    factor_of, own = 1.0, jax.random.fold_in(stream_key, 6)
    for dim, shards_of in shards:
        steps = jnp.exp(jax.random.uniform(jax.random.fold_in(own, dim), (shards_of,), jnp.float32, least / len(shards), top_value / len(shards)))
        factor_of = factor_of * jnp.repeat(steps, dims[dim] // shards_of).reshape([-1 if axis == dim else 1 for axis in range(len(dims))])
    return factor_of


def setup_inputs(seed: int = 0) -> dict:
    key_of = jax.random.split(jax.random.key(seed), 6)
    return {
        "data": jnp.clip(48.0 * jax.random.uniform(key_of[0], (2, G, NC), jnp.float32) ** level_of(key_of[0], (2, G, NC), ((0, 2), (1, 4), (2, 4)), -0.2, 0.2), 0.0, 48.0).astype(jnp.bfloat16),
        "shared_w": jnp.clip(jnp.exp(math.log(2.0) - 6.9077552 * jax.random.uniform(key_of[1], (G, K), jnp.float32) ** level_of(key_of[1], (G, K), ((0, 16),), -0.2, 0.2)), 0.002, 2.0),
        "specific_v": jnp.clip(jnp.exp(math.log(0.5) - 6.9077552 * jax.random.uniform(key_of[2], (2, G, K), jnp.float32) ** level_of(key_of[2], (2, G, K), ((0, 2), (1, 16)), -0.2, 0.2)), 0.0005, 0.5),
        "factor_h": jnp.clip(jnp.exp(math.log(1.0) - 4.6051702 * jax.random.uniform(key_of[3], (2, K, NC), jnp.float32) ** level_of(key_of[3], (2, K, NC), ((0, 2), (2, 4)), -0.2, 0.2)), 0.01, 1.0),
        "cell_count": draw_cell_count(jax.random.fold_in(key_of[5], 71), 0),
    }


LAMBDA = 5.0
TINY = 1e-6
HIGH = lax.Precision.HIGHEST


def sweep_rows(state, gram, drive, live, width):
    def one(index, state):
        start = jnp.asarray(index).astype(jnp.int32) * width
        rows = lax.dynamic_slice_in_dim(gram, start, width, 0)
        grad = jnp.dot(rows, state, precision=HIGH) - lax.dynamic_slice_in_dim(drive, start, width, 0)
        block = lax.dynamic_slice_in_dim(rows, start, width, 1)
        scale = jnp.sum(jnp.abs(block), axis=1) + TINY
        current = lax.dynamic_slice_in_dim(state, start, width, 0)
        fresh = jnp.maximum(current - grad / scale[:, None], 0.0) * live[None, :]
        return lax.dynamic_update_slice_in_dim(state, fresh, start, 0)
    for sweep in range(SWEEPS):
        state = lax.fori_loop(0, K // width, one, state)
    return state


def sweep_columns(matrix, offset, quad, target, factor, width):
    def one(index, matrix):
        start = jnp.asarray(index).astype(jnp.int32) * width
        cols = lax.dynamic_slice_in_dim(quad, start, width, 1)
        grad = jnp.dot(factor * matrix + offset, cols, precision=HIGH) - lax.dynamic_slice_in_dim(target, start, width, 1)
        block = lax.dynamic_slice_in_dim(cols, start, width, 0)
        scale = factor * jnp.sum(jnp.abs(block), axis=0) + TINY
        current = lax.dynamic_slice_in_dim(matrix, start, width, 1)
        fresh = jnp.maximum(current - grad / scale[None, :], 0.0)
        return lax.dynamic_update_slice_in_dim(matrix, fresh, start, 1)
    for sweep in range(SWEEPS):
        matrix = lax.fori_loop(0, K // width, one, matrix)
    return matrix


def reference(data, shared_w, specific_v, factor_h, cell_count):
    slots = jnp.arange(NC, dtype=jnp.int32)
    new_v = []
    new_h = []
    rest = jnp.zeros(shared_w.shape, jnp.float32)
    cross_sum = jnp.zeros((K, K), jnp.float32)
    for group in range(2):
        expr = data[group]
        mix = (shared_w + specific_v[group]).astype(jnp.bfloat16)
        own = specific_v[group].astype(jnp.bfloat16)
        gram = jnp.dot(mix.T, mix, preferred_element_type=jnp.float32) + LAMBDA * jnp.dot(own.T, own, preferred_element_type=jnp.float32)
        drive = jnp.dot(mix.T, expr, preferred_element_type=jnp.float32)
        live = (slots < cell_count[group]).astype(jnp.float32)
        state = sweep_rows(factor_h[group], gram, drive, live, KB)
        rounded = state.astype(jnp.bfloat16)
        proj = jnp.dot(expr, rounded.T, preferred_element_type=jnp.float32)
        cross = jnp.dot(rounded, rounded.T, preferred_element_type=jnp.float32)
        loading = sweep_columns(specific_v[group], shared_w, cross, proj, 1.0 + LAMBDA, KB)
        rest = rest + proj - jnp.dot(loading, cross, precision=HIGH)
        cross_sum = cross_sum + cross
        new_v.append(loading)
        new_h.append(state)
    new_w = sweep_columns(shared_w, jnp.zeros(shared_w.shape, jnp.float32), cross_sum, rest, 1.0, KB)
    return new_w, jnp.stack(new_v), jnp.stack(new_h)
```

```python
import jax
import jax.numpy as jnp
from jax import lax
from jax.experimental import pallas as pl
from jax.experimental.pallas import tpu as pltpu
from jax.sharding import PartitionSpec as P

K = 256
KB = 32
NB = K // KB
SWEEPS = 4


LAMBDA = 5.0
TINY = 1e-06
HIGH = lax.Precision.HIGHEST
F32 = jnp.float32
BF16 = jnp.bfloat16


def contract_rows(left, right):
    return lax.dot_general(
        left, right, (((0,), (0,)), ((), ())), preferred_element_type=jnp.float32
    )


def contract_cols(left, right):
    return lax.dot_general(
        left, right, (((1,), (1,)), ((), ())), preferred_element_type=jnp.float32
    )


def product(left, right):
    return lax.dot_general(
        left, right, (((1,), (0,)), ((), ())), preferred_element_type=jnp.float32
    )


def split(x):
    high = x.astype(BF16)
    return high, (x - high.astype(F32)).astype(BF16)


def prepare(quad, stack_ref, inv_ref, factor):
    row = lax.broadcasted_iota(jnp.int32, (K, K), 0) // KB
    col = lax.broadcasted_iota(jnp.int32, (K, K), 1) // KB
    total = jnp.sum(jnp.where(row == col, jnp.abs(quad), 0.0), axis=1, keepdims=True)
    inv_ref[...] = 1.0 / (factor * total + TINY)
    high, low = split(quad)
    for b in range(NB):
        h = high[:, b * KB : (b + 1) * KB]
        stack_ref[b] = jnp.concatenate([h, h, low[:, b * KB : (b + 1) * KB]], axis=1)
    return high, low


def full_product(high, low, x):
    x_high, x_low = split(x)
    return product(high, x_high) + product(high, x_low) + product(low, x_high)


def sweep(x_ref, p_ref, c_ref, stack_ref, inv_ref, factor, live):
    def one(_, carry):
        for b in range(NB):
            rows = pl.ds(b * KB, KB)
            old = x_ref[rows, :]
            grad = p_ref[rows, :]
            if c_ref is not None:
                grad = factor * grad + c_ref[rows, :]
            new = jnp.maximum(old - grad * inv_ref[rows, :], 0.0)
            if live is not None:
                new = new * live
            high, low = split(new - old)
            x_ref[rows, :] = new
            p_ref[...] += product(stack_ref[b], jnp.concatenate([high, low, high], axis=0))
        return carry

    lax.fori_loop(0, SWEEPS, one, 0)


def h_kernel(gram_ref, drive_ref, state_ref, live_ref, out_ref, round_ref, stack, inv, p):
    high, low = prepare(gram_ref[...], stack, inv, 1.0)
    out_ref[...] = state_ref[...]
    p[...] = full_product(high, low, state_ref[...]) - drive_ref[...]
    sweep(out_ref, p, None, stack, inv, 1.0, live_ref[...])
    round_ref[...] = out_ref[...].astype(BF16)


def cross_kernel(*refs):
    pieces, out_ref = refs[:-1], refs[-1]
    total = contract_cols(pieces[0][...], pieces[0][...])
    for piece in pieces[1:]:
        total += contract_cols(piece[...], piece[...])
    out_ref[...] = total


def v_kernel(parts, *refs):
    factors, owned = refs[:parts], refs[parts : 2 * parts]
    cross_ref, v_ref, w_ref, out_ref, rest_ref, stack, inv, x, p, c = refs[2 * parts :]
    high, low = prepare(cross_ref[...], stack, inv, 1.0 + LAMBDA)
    base = full_product(high, low, w_ref[...].T)
    for factor, piece in zip(factors, owned):
        base -= contract_cols(factor[...], piece[...])
    c[...] = base
    x[...] = v_ref[...].T
    p[...] = full_product(high, low, x[...])
    sweep(x, p, c, stack, inv, 1.0 + LAMBDA, None)
    rest_ref[...] = p[...] + c[...]
    out_ref[...] = x[...].T


def w_kernel(cross_a, cross_b, rest_a, rest_b, w_ref, out_ref, stack, inv, x, p):
    prepare(cross_a[...] + cross_b[...], stack, inv, 1.0)
    x[...] = w_ref[...].T
    p[...] = rest_a[...] + rest_b[...]
    sweep(x, p, None, stack, inv, 1.0, None)
    out_ref[...] = x[...].T.astype(BF16)


def scratch(n, count):
    return [pltpu.VMEM((NB, K, 3 * KB), BF16), pltpu.VMEM((K, 1), F32)] + [
        pltpu.VMEM((K, n), F32) for _ in range(count)
    ]


def cost(work):
    return pl.CostEstimate(flops=int(work), bytes_accessed=1 << 20, transcendentals=0)


def h_call(gram, drive, state, live):
    n = state.shape[1]
    return pl.pallas_call(
        h_kernel,
        out_shape=(jax.ShapeDtypeStruct((K, n), F32), jax.ShapeDtypeStruct((K, n), BF16)),
        scratch_shapes=scratch(n, 1),
        cost_estimate=cost(8e9),
        name="h_sweep",
    )(gram, drive, state, live)


def cross_call(pieces):
    return pl.pallas_call(
        cross_kernel,
        out_shape=jax.ShapeDtypeStruct((K, K), F32),
        cost_estimate=cost(5e8),
        name="cross",
    )(*pieces)


def v_call(factors, owned, cross, v, w):
    n = v.shape[0]
    parts = len(factors)

    def kernel(*refs):
        v_kernel(parts, *refs)

    return pl.pallas_call(
        kernel,
        out_shape=(jax.ShapeDtypeStruct((n, K), F32), jax.ShapeDtypeStruct((K, n), F32)),
        scratch_shapes=scratch(n, 3),
        cost_estimate=cost(1e10),
        name="v_sweep",
    )(*factors, *owned, cross, v, w)


def w_call(cross_a, cross_b, rest_a, rest_b, w):
    n = w.shape[0]
    return pl.pallas_call(
        w_kernel,
        out_shape=jax.ShapeDtypeStruct((n, K), BF16),
        scratch_shapes=scratch(n, 2),
        cost_estimate=cost(1e10),
        name="w_sweep",
    )(cross_a, cross_b, rest_a, rest_b, w)


def swap(x, axis, size, bit):
    return lax.ppermute(x, axis, [(i, i ^ bit) for i in range(size)])


def shift(x, axis, size, step):
    return lax.ppermute(x, axis, [(i, (i + step) % size) for i in range(size)])


def after(x, *others):
    return lax.optimization_barrier((x,) + others)[0]


def rows(x, start, count):
    return lax.dynamic_slice_in_dim(x, start, count, 0)


def pair(mine, other, first):
    return jnp.concatenate([jnp.where(first, mine, other), jnp.where(first, other, mine)], axis=0)


def line_shards(data, shared_w, specific_v, factor_h, cell_count):
    expr = data[0]
    v = specific_v[0]
    cells = expr.shape[1]
    own_genes = shared_w.shape[0]
    half = own_genes // 2
    grp = lax.axis_index("grp")
    gene = lax.axis_index("gene")
    z = lax.axis_index("cell")
    y, core = gene // 2, gene % 2
    mix = (shared_w + v).astype(BF16)
    own = v.astype(BF16)

    up1 = lax.ppermute(mix, "cell", [(0, 1), (1, 2), (2, 3)])
    down1 = lax.ppermute(mix, "cell", [(3, 2), (2, 1), (1, 0)])
    up2 = lax.ppermute(up1, "cell", [(1, 2), (2, 3)])
    down2 = lax.ppermute(down1, "cell", [(2, 1), (1, 0)])
    far2 = jnp.where(z >= 2, up2, down2)
    far3 = lax.ppermute(far2, "cell", [(2, 3), (1, 0)])

    gram = contract_rows(mix, mix) + LAMBDA * contract_rows(own, own)
    gram = gram + swap(gram, "gene", 4, 1)
    keep = rows(gram, y * (K // 2), K // 2) + swap(rows(gram, (1 - y) * (K // 2), K // 2), "gene", 4, 2)
    quarter = rows(keep, core * (K // 4), K // 4)
    quarter = quarter + shift(quarter, "cell", 4, 1) + shift(quarter, "cell", 4, 2) + shift(quarter, "cell", 4, 3)
    gram = pair(quarter, swap(quarter, "gene", 4, 1), core == 0)
    gram = pair(gram, swap(gram, "gene", 4, 2), y == 0)

    mine, theirs = grp * half, (1 - grp) * half
    def exchange(source, start):
        pieces = [rows(source, z * own_genes + start, half)]
        for step in (1, 2, 3):
            piece = rows(source, ((z + step) % 4) * own_genes + start, half)
            pieces.append(shift(piece, "cell", 4, step))
        return pieces
    expr_a = after(expr, up2, down2)
    owned_a = exchange(expr_a, theirs)
    expr_b = after(expr, far3)
    owned_b = exchange(expr_b, mine)

    def term(piece, source):
        return contract_rows(piece, rows(expr, source * own_genes, own_genes))
    drive = term(mix, z) + term(up1, jnp.maximum(z - 1, 0)) + term(down1, jnp.minimum(z + 1, 3))
    drive = drive + term(far2, z ^ 2) + term(far3, 3 - z)
    drive = drive + swap(drive, "gene", 4, 1)
    drive = drive + swap(drive, "gene", 4, 2)

    slots = z * cells + jnp.arange(cells, dtype=jnp.int32)
    live = (slots < cell_count[0]).astype(F32)[None, :]
    state, rounded = h_call(gram, drive, factor_h[0], live)

    factors = [rounded] + [shift(rounded, "cell", 4, step) for step in (1, 2, 3)]
    cross = cross_call(factors)
    cross_other = swap(cross, "grp", 2, 1)
    w_a, w_b = rows(shared_w, theirs, half), rows(shared_w, mine, half)
    v_a, v_b = rows(v, theirs, half), rows(v, mine, half)
    new_a, rest_a = v_call(factors, owned_a, cross, v_a, w_a)
    rest_other = swap(rest_a, "grp", 2, 1)
    new_b, rest_b = v_call(factors, owned_b, cross, v_b, w_b)
    w_mine = w_call(cross, cross_other, rest_b, rest_other, w_b)
    w_theirs = swap(w_mine, "grp", 2, 1)
    new_w = pair(w_mine, w_theirs, grp == 0).astype(F32)
    new_v = pair(new_b, new_a, grp == 0)
    return (new_w, new_v[None], state[None])


def sweep_rows(state, gram, drive, live, width):

    def one(index, state):
        start = jnp.asarray(index).astype(jnp.int32) * width
        rows = lax.dynamic_slice_in_dim(gram, start, width, 0)
        grad = jnp.dot(rows, state, precision=HIGH) - lax.dynamic_slice_in_dim(
            drive, start, width, 0
        )
        block = lax.dynamic_slice_in_dim(rows, start, width, 1)
        scale = jnp.sum(jnp.abs(block), axis=1) + TINY
        current = lax.dynamic_slice_in_dim(state, start, width, 0)
        fresh = jnp.maximum(current - grad / scale[:, None], 0.0) * live[None, :]
        return lax.dynamic_update_slice_in_dim(state, fresh, start, 0)

    for sweep in range(SWEEPS):
        state = lax.fori_loop(0, K // width, one, state)
    return state


def sweep_columns(matrix, offset, quad, target, factor, width):

    def one(index, matrix):
        start = jnp.asarray(index).astype(jnp.int32) * width
        cols = lax.dynamic_slice_in_dim(quad, start, width, 1)
        grad = jnp.dot(factor * matrix + offset, cols, precision=HIGH) - lax.dynamic_slice_in_dim(
            target, start, width, 1
        )
        block = lax.dynamic_slice_in_dim(cols, start, width, 0)
        scale = factor * jnp.sum(jnp.abs(block), axis=0) + TINY
        current = lax.dynamic_slice_in_dim(matrix, start, width, 1)
        fresh = jnp.maximum(current - grad / scale[None, :], 0.0)
        return lax.dynamic_update_slice_in_dim(matrix, fresh, start, 1)

    for sweep in range(SWEEPS):
        matrix = lax.fori_loop(0, K // width, one, matrix)
    return matrix


def general_shards(data, shared_w, specific_v, factor_h, cell_count):
    expr = data[0]
    loading = specific_v[0]
    state = factor_h[0]
    cells = expr.shape[1]
    mix = (shared_w + loading).astype(BF16)
    own = loading.astype(BF16)
    part_mix = lax.all_gather(mix, "cell", axis=0, tiled=True)
    drive = lax.psum(contract_rows(part_mix, expr), "gene")
    gram = contract_rows(mix, mix) + LAMBDA * contract_rows(own, own)
    gram = lax.psum(gram, ("gene", "cell"))
    slots = lax.axis_index("cell") * cells + jnp.arange(cells, dtype=jnp.int32)
    live = (slots < cell_count[0]).astype(F32)
    state = sweep_rows(state, gram, drive, live, KB)
    rounded = state.astype(BF16)
    owned = lax.all_to_all(expr, "cell", split_axis=0, concat_axis=1, tiled=True)
    factors = lax.all_gather(rounded, "cell", axis=1, tiled=True)
    proj = contract_cols(owned, factors)
    cross = contract_cols(factors, factors)
    loading = sweep_columns(loading, shared_w, cross, proj, 1.0 + LAMBDA, KB)
    rest = proj - jnp.dot(loading, cross, precision=HIGH)
    rest, cross_sum = lax.psum((rest, cross), "grp")
    new_w = sweep_columns(shared_w, jnp.zeros(shared_w.shape, F32), cross_sum, rest, 1.0, KB)
    return (new_w, loading[None], state[None])


def solution(mesh):
    in_specs = (
        P("grp", "gene", "cell"),
        P(("gene", "cell"), None),
        P("grp", ("gene", "cell"), None),
        P("grp", None, "cell"),
        P("grp"),
    )
    out_specs = (
        P(("gene", "cell"), None),
        P("grp", ("gene", "cell"), None),
        P("grp", None, "cell"),
    )
    sizes = (mesh.shape["grp"], mesh.shape["gene"], mesh.shape["cell"])
    shards = line_shards if sizes == (2, 4, 4) else general_shards
    return jax.shard_map(shards, mesh=mesh, in_specs=in_specs, out_specs=out_specs, check_vma=False)
```

```python
import jax
import jax.numpy as jnp
from jax import lax
from jax.experimental import pallas as pl
from jax.experimental.pallas import tpu as pltpu
from jax.sharding import PartitionSpec as P

K = 256
KB = 32
NB = K // KB
SWEEPS = 4


LAMBDA = 5.0
TINY = 1e-06
HIGH = lax.Precision.HIGHEST
F32 = jnp.float32
BF16 = jnp.bfloat16


def contract_rows(left, right):
    return lax.dot_general(
        left, right, (((0,), (0,)), ((), ())), preferred_element_type=jnp.float32
    )


def contract_cols(left, right):
    return lax.dot_general(
        left, right, (((1,), (1,)), ((), ())), preferred_element_type=jnp.float32
    )


def product(left, right):
    return lax.dot_general(
        left, right, (((1,), (0,)), ((), ())), preferred_element_type=jnp.float32
    )


def split(x):
    high = x.astype(BF16)
    return high, (x - high.astype(F32)).astype(BF16)


def prepare(quad, stack_ref, inv_ref, factor):
    row = lax.broadcasted_iota(jnp.int32, (K, K), 0) // KB
    col = lax.broadcasted_iota(jnp.int32, (K, K), 1) // KB
    total = jnp.sum(jnp.where(row == col, jnp.abs(quad), 0.0), axis=1, keepdims=True)
    inv_ref[...] = 1.0 / (factor * total + TINY)
    high, low = split(quad)
    for b in range(NB):
        h = high[:, b * KB : (b + 1) * KB]
        cols = jnp.concatenate([h, h, low[:, b * KB : (b + 1) * KB]], axis=1)
        start = (b + 1) % NB * KB
        if start:
            cols = jnp.concatenate([cols[start:], cols[:start]], axis=0)
        stack_ref[b] = cols
    return high, low


def full_product(high, low, x):
    x_high, x_low = split(x)
    return product(high, x_high) + product(high, x_low) + product(low, x_high)


def sweep(x_ref, p_ref, c_ref, stack_ref, inv_ref, factor, live):
    def one(_, carry):
        for b in range(NB):
            rows = pl.ds(b * KB, KB)
            old = x_ref[rows, :]
            grad = p_ref[rows, :]
            if c_ref is not None:
                grad = factor * grad + c_ref[rows, :]
            new = jnp.maximum(old - grad * inv_ref[rows, :], 0.0)
            if live is not None:
                new = new * live
            high, low = split(new - old)
            x_ref[rows, :] = new
            change = product(stack_ref[b], jnp.concatenate([high, low, high], axis=0))
            for i in range(NB):
                p_ref[pl.ds((b + 1 + i) % NB * KB, KB), :] += change[i * KB : (i + 1) * KB]
        return carry

    lax.fori_loop(0, SWEEPS, one, 0)


def halves(mine, other, first):
    return jnp.concatenate([jnp.where(first, mine, other), jnp.where(first, other, mine)], axis=0)


def h_kernel(
    q_ref, q_core_ref, q_y_ref, drive_ref, drive_core_ref, state_ref, live_ref,
    out_ref, round_ref, half_ref, stack, inv, p,
):
    gene = lax.axis_index("gene")
    y, core = gene // 2 == 0, gene % 2 == 0
    near = halves(q_ref[...], q_core_ref[...], core)
    far = q_y_ref[...]
    far = halves(far[: K // 4], far[K // 4 :], core)
    high, low = prepare(halves(near, far, y), stack, inv, 1.0)
    out_ref[...] = state_ref[...]
    drive = halves(drive_ref[...], drive_core_ref[...], core)
    p[...] = full_product(high, low, state_ref[...]) - drive
    sweep(out_ref, p, None, stack, inv, 1.0, live_ref[...])
    rounded = out_ref[...].astype(BF16)
    round_ref[...] = rounded
    half_ref[...] = jnp.where(core, rounded[: K // 2], rounded[K // 2 :])


def cross_kernel(own_ref, *refs):
    mine, other, (out_ref, all_ref) = refs[:3], refs[3:6], refs[6:]
    core = lax.axis_index("gene") % 2 == 0
    total = contract_cols(own_ref[...], own_ref[...])
    all_ref[0] = own_ref[...]
    for k in range(3):
        factor = halves(mine[k][...], other[k][...], core)
        total += contract_cols(factor, factor)
        all_ref[k + 1] = factor
    out_ref[...] = total


def v_kernel(factors, own_ref, *refs):
    middle, end = refs[:3], refs[3:6]
    cross_ref, v_ref, w_ref, out_ref, rest_ref, stack, inv, x, p, c = refs[6:]
    z = lax.axis_index("cell")
    at_end = (z == 0) | (z == 3)
    high, low = prepare(cross_ref[...], stack, inv, 1.0 + LAMBDA)
    base = full_product(high, low, w_ref[...].T) - contract_cols(factors[0], own_ref[...])
    for k in range(3):
        piece = jnp.where(at_end, end[k][...], middle[k][...])
        base -= contract_cols(factors[k + 1], piece)
    c[...] = base
    x[...] = v_ref[...].T
    p[...] = full_product(high, low, x[...])
    sweep(x, p, c, stack, inv, 1.0 + LAMBDA, None)
    rest_ref[...] = p[...] + c[...]
    out_ref[...] = x[...].T


def w_kernel(cross_a, cross_b, rest_a, rest_b, w_ref, out_ref, stack, inv, x, p):
    prepare(cross_a[...] + cross_b[...], stack, inv, 1.0)
    x[...] = w_ref[...].T
    p[...] = rest_a[...] + rest_b[...]
    sweep(x, p, None, stack, inv, 1.0, None)
    out_ref[...] = x[...].T.astype(BF16)


def scratch(n, count):
    return [pltpu.VMEM((NB, K, 3 * KB), BF16), pltpu.VMEM((K, 1), F32)] + [
        pltpu.VMEM((K, n), F32) for _ in range(count)
    ]


def cost(work):
    return pl.CostEstimate(flops=int(work), bytes_accessed=1 << 20, transcendentals=0)


def h_call(quarter, quarter_core, quarter_y, drive, drive_core, state, live):
    n = state.shape[1]
    return pl.pallas_call(
        h_kernel,
        out_shape=(
            jax.ShapeDtypeStruct((K, n), F32),
            jax.ShapeDtypeStruct((K, n), BF16),
            jax.ShapeDtypeStruct((K // 2, n), BF16),
        ),
        scratch_shapes=scratch(n, 1),
        cost_estimate=cost(8e9),
        name="h_sweep",
    )(quarter, quarter_core, quarter_y, drive, drive_core, state, live)


def cross_call(own, mine, other):
    n = own.shape[1]
    return pl.pallas_call(
        cross_kernel,
        out_shape=(jax.ShapeDtypeStruct((K, K), F32), jax.ShapeDtypeStruct((4, K, n), BF16)),
        cost_estimate=cost(5e8),
        name="cross",
    )(own, *mine, *other)


def v_call(factors, own, middle, end, cross, v, w):
    n = v.shape[0]
    return pl.pallas_call(
        v_kernel,
        out_shape=(jax.ShapeDtypeStruct((n, K), F32), jax.ShapeDtypeStruct((K, n), F32)),
        scratch_shapes=scratch(n, 3),
        cost_estimate=cost(1e10),
        name="v_sweep",
    )(factors, own, *middle, *end, cross, v, w)


def w_call(cross_a, cross_b, rest_a, rest_b, w):
    n = w.shape[0]
    return pl.pallas_call(
        w_kernel,
        out_shape=jax.ShapeDtypeStruct((n, K), BF16),
        scratch_shapes=scratch(n, 2),
        cost_estimate=cost(1e10),
        name="w_sweep",
    )(cross_a, cross_b, rest_a, rest_b, w)


def send(name, x, axis, perm):
    with jax.named_scope(name):
        return lax.ppermute(x, axis, perm)


def swap(name, x, axis, size, bit):
    return send(name, x, axis, [(i, i ^ bit) for i in range(size)])


def after(x, *others):
    return lax.optimization_barrier((x,) + others)[0]


def rows(x, start, count):
    return lax.dynamic_slice_in_dim(x, start, count, 0)


def pair(mine, other, first):
    return jnp.concatenate([jnp.where(first, mine, other), jnp.where(first, other, mine)], axis=0)


def line_shards(data, shared_w, specific_v, factor_h, cell_count):
    expr = data[0]
    v = specific_v[0]
    cells = expr.shape[1]
    count = shared_w.shape[0]
    half = count // 2
    grp = lax.axis_index("grp")
    gene = lax.axis_index("gene")
    z = lax.axis_index("cell")
    y, core = gene // 2, gene % 2
    end = (z == 0) | (z == 3)
    mix = (shared_w + v).astype(BF16)
    own = v.astype(BF16)

    def block(owner):
        return rows(expr, owner * count, count)

    up, down = [(0, 1), (1, 2), (2, 3)], [(3, 2), (2, 1), (1, 0)]
    up1 = send("up1", mix, "cell", up)
    down1 = send("down1", mix, "cell", down)
    up2 = send("up2", jnp.where(z == 0, block(1), up1), "cell", up)
    down2 = send("down2", jnp.where(z == 3, block(2), down1), "cell", down)
    far2 = jnp.where(z >= 2, up2, down2)
    block1 = jnp.where(z == 1, up2, down2)
    across = jnp.where(end, block(jnp.where(z == 0, 2, 1)), far2)
    got3 = send("far3", across, "cell", [(0, 2), (1, 0), (2, 3), (3, 1)])
    block2 = got3
    far3 = jnp.where(end, got3, jnp.zeros_like(got3))
    block3 = send("mid", after(block(z ^ 3), far2), "cell", [(1, 2), (2, 1)])

    gram = contract_rows(mix, mix) + LAMBDA * contract_rows(own, own)
    gram = gram + swap("gram_core", gram, "gene", 4, 1)
    keep = rows(gram, y * (K // 2), K // 2)
    keep = keep + swap("gram_y", rows(gram, (1 - y) * (K // 2), K // 2), "gene", 4, 2)
    quarter = rows(keep, core * (K // 4), K // 4)
    sent = after(quarter, far2)
    for k in (1, 2, 3):
        quarter = quarter + swap("gram_z%d" % k, sent, "cell", 4, k)
    quarter_core = swap("gram_core2", quarter, "gene", 4, 1)
    quarter_y = swap("gram_y2", jnp.concatenate([quarter, quarter_core], axis=0), "gene", 4, 2)

    def term(piece, owner):
        return contract_rows(piece, block(owner))
    drive = term(mix, z) + term(up1, jnp.maximum(z - 1, 0)) + term(down1, jnp.minimum(z + 1, 3))
    drive = drive + term(far2, z ^ 2) + term(far3, 3 - z)
    drive = drive + swap("drive_core", drive, "gene", 4, 1)
    drive = rows(drive, core * (K // 2), K // 2)
    drive = drive + swap("drive_y", drive, "gene", 4, 2)
    drive_core = swap("drive_core2", drive, "gene", 4, 1)

    slots = z * cells + jnp.arange(cells, dtype=jnp.int32)
    live = (slots < cell_count[0]).astype(F32)[None, :]
    state, rounded, part = h_call(quarter, quarter_core, quarter_y, drive, drive_core, factor_h[0], live)

    mine, theirs = grp * half, (1 - grp) * half
    perms = ([(1, 0), (2, 3)], [(2, 0), (1, 3)], [(3, 0), (0, 3)])
    def to_ends(name, source, start):
        return [
            send(name + str(k), rows(source, (z ^ k) * count + start, half), "cell", perms[k - 1])
            for k in (1, 2, 3)
        ]
    ends_a = to_ends("ends_a", after(expr, got3), theirs)
    parts = [swap("factors%d" % k, part, "cell", 4, k) for k in (1, 2, 3)]
    ends_b = to_ends("ends_b", after(expr, part), mine)
    others = [swap("factors_core%d" % k, parts[k - 1], "gene", 4, 1) for k in (1, 2, 3)]
    cross, factors = cross_call(rounded, parts, others)
    cross_other = swap("cross", cross, "grp", 2, 1)

    def v_side(start, ends):
        middle = [rows(b, start, half) for b in (block1, block2, block3)]
        own = rows(expr, z * count + start, half)
        return v_call(factors, own, middle, ends, cross, rows(v, start, half), rows(shared_w, start, half))
    new_a, rest_a = v_side(theirs, ends_a)
    rest_other = swap("rest", rest_a, "grp", 2, 1)
    new_b, rest_b = v_side(mine, ends_b)
    w_mine = w_call(cross, cross_other, rest_b, rest_other, rows(shared_w, mine, half))
    w_theirs = swap("new_w", w_mine, "grp", 2, 1)
    new_w = pair(w_mine, w_theirs, grp == 0).astype(F32)
    new_v = pair(new_b, new_a, grp == 0)
    return (new_w, new_v[None], state[None])


def sweep_rows(state, gram, drive, live, width):

    def one(index, state):
        start = jnp.asarray(index).astype(jnp.int32) * width
        rows = lax.dynamic_slice_in_dim(gram, start, width, 0)
        grad = jnp.dot(rows, state, precision=HIGH) - lax.dynamic_slice_in_dim(
            drive, start, width, 0
        )
        block = lax.dynamic_slice_in_dim(rows, start, width, 1)
        scale = jnp.sum(jnp.abs(block), axis=1) + TINY
        current = lax.dynamic_slice_in_dim(state, start, width, 0)
        fresh = jnp.maximum(current - grad / scale[:, None], 0.0) * live[None, :]
        return lax.dynamic_update_slice_in_dim(state, fresh, start, 0)

    for sweep in range(SWEEPS):
        state = lax.fori_loop(0, K // width, one, state)
    return state


def sweep_columns(matrix, offset, quad, target, factor, width):

    def one(index, matrix):
        start = jnp.asarray(index).astype(jnp.int32) * width
        cols = lax.dynamic_slice_in_dim(quad, start, width, 1)
        grad = jnp.dot(factor * matrix + offset, cols, precision=HIGH) - lax.dynamic_slice_in_dim(
            target, start, width, 1
        )
        block = lax.dynamic_slice_in_dim(cols, start, width, 0)
        scale = factor * jnp.sum(jnp.abs(block), axis=0) + TINY
        current = lax.dynamic_slice_in_dim(matrix, start, width, 1)
        fresh = jnp.maximum(current - grad / scale[None, :], 0.0)
        return lax.dynamic_update_slice_in_dim(matrix, fresh, start, 1)

    for sweep in range(SWEEPS):
        matrix = lax.fori_loop(0, K // width, one, matrix)
    return matrix


def general_shards(data, shared_w, specific_v, factor_h, cell_count):
    expr = data[0]
    loading = specific_v[0]
    state = factor_h[0]
    cells = expr.shape[1]
    mix = (shared_w + loading).astype(BF16)
    own = loading.astype(BF16)
    part_mix = lax.all_gather(mix, "cell", axis=0, tiled=True)
    drive = lax.psum(contract_rows(part_mix, expr), "gene")
    gram = contract_rows(mix, mix) + LAMBDA * contract_rows(own, own)
    gram = lax.psum(gram, ("gene", "cell"))
    slots = lax.axis_index("cell") * cells + jnp.arange(cells, dtype=jnp.int32)
    live = (slots < cell_count[0]).astype(F32)
    state = sweep_rows(state, gram, drive, live, KB)
    rounded = state.astype(BF16)
    owned = lax.all_to_all(expr, "cell", split_axis=0, concat_axis=1, tiled=True)
    factors = lax.all_gather(rounded, "cell", axis=1, tiled=True)
    proj = contract_cols(owned, factors)
    cross = contract_cols(factors, factors)
    loading = sweep_columns(loading, shared_w, cross, proj, 1.0 + LAMBDA, KB)
    rest = proj - jnp.dot(loading, cross, precision=HIGH)
    rest, cross_sum = lax.psum((rest, cross), "grp")
    new_w = sweep_columns(shared_w, jnp.zeros(shared_w.shape, F32), cross_sum, rest, 1.0, KB)
    return (new_w, loading[None], state[None])


def solution(mesh):
    in_specs = (
        P("grp", "gene", "cell"),
        P(("gene", "cell"), None),
        P("grp", ("gene", "cell"), None),
        P("grp", None, "cell"),
        P("grp"),
    )
    out_specs = (
        P(("gene", "cell"), None),
        P("grp", ("gene", "cell"), None),
        P("grp", None, "cell"),
    )
    sizes = (mesh.shape["grp"], mesh.shape["gene"], mesh.shape["cell"])
    shards = line_shards if sizes == (2, 4, 4) else general_shards
    return jax.shard_map(shards, mesh=mesh, in_specs=in_specs, out_specs=out_specs, check_vma=False)
```
